256 devices in a mesh: page: 32 (over z, x), feat: 8 (over y, core).
Axes of the slice: x: 4, y: 4, z: 8, core: 2. Of those that a mesh axis runs over, the one named last changes fastest.
Arguments:
- queries: bfloat16 [256, 4096], P('page', 'feat')
- fresh_token_keys: bfloat16 [256, 2048], P('page', 'feat')
- fresh_token_values: bfloat16 [256, 2048], P('page', 'feat'), may hold values from -6 to 6
- paged_keys: bfloat16 [512, 256, 2048], P('page', None, 'feat'), may hold values from -6 to 6
- paged_values: bfloat16 [512, 256, 2048], P('page', None, 'feat'), may hold values from -6 to 6
- block_tables: int32 [256, 8], replicated, may hold values from -1 to 511, as said below
- parents: int32 [256], replicated, may hold values from 0 to 255, as said below
- prompt_lengths: int32 [32], replicated, may hold values from 1 to 2047, as said below
- stream: bfloat16 [256, 4608], P(('page', 'feat'))
- output_matrix: bfloat16 [4608, 4096], P(None, 'feat')
- attention_gain: bfloat16 [4608], replicated, may hold values from 0.5 to 1.5
- feedforward_gain: bfloat16 [4608], replicated, may hold values from 0.5 to 1.5
- gate_matrix: bfloat16 [36864, 4608], P(('page', 'feat')), may hold values from -0.09375 to 0.09375
- linear_matrix: bfloat16 [36864, 4608], P(('page', 'feat')), may hold values from -0.09375 to 0.09375
- down_matrix: bfloat16 [36864, 4608], P(('page', 'feat'))
- closing_gain: bfloat16 [4608], replicated, may hold values from 0.5 to 1.5
Outputs:
- layer_output: bfloat16 [256, 4608], P(('page', 'feat'))
The draws below stay inside these ranges and needn't reach their ends.
Inputs may be any that keep to these rules, and one draw needn't show every extreme that they name: `block_tables`: row r's table lists the page slots of its blocks in order; entries from ceil(prompt_lengths[r // 8] / 256) on are -1. Rows of one prompt list the same slots for all but their last listed block, which is each row's own. A slot is listed by the rows of one prompt only, and at most once in a row. `prompt_lengths`: the new token of each prompt's rows stands at this position. `parents`: the parent of row r is a row of the same prompt, from 8 * (r // 8) to that plus 8 - 1.
All inputs are finite; a program needn't handle non-finite values.
Results may differ from the reference program's by a relative error of at most 0.0095.
Values may be sent and summed in bfloat16 or wider, within the bound.
No kernel may reach another device: no remote copies, remote signals or barrier semaphores. Data moves between devices by JAX's collectives and lax.ppermute only.
A program may use at most 64 MiB of HBM per device.

```python
import math
import jax
import jax.numpy as jnp
from jax import lax

D = 4608
FF = 36864
QUERY_HEADS = 32
KEY_VALUE_HEADS = 16
HEAD_DIM_SIZE = 128
QSCALAR = 144
SOFTCAP = 50
PAGE_TOKENS = 256
TABLE_BLOCKS = 8
BEAMS = 8
PAGE_SLOTS = 512
PROMPTS = 32
BEAM_ROW_COUNT = 256


def table_entries(key, shape):
    return jax.random.normal(key, shape, jnp.float32)


def spread(key, count):
    uniform_part = jax.random.uniform(key, (count,), jnp.float32)
    return jnp.exp(math.log(6.0) * (uniform_part - 0.5))


def draw_stream(key, part):
    random_subkeys = jax.random.split(jax.random.fold_in(key, 21), 3)
    columns = spread(random_subkeys[0], D)
    row_scale = spread(random_subkeys[1], BEAM_ROW_COUNT)
    values = table_entries(random_subkeys[2], (BEAM_ROW_COUNT, D)) * row_scale[:, None]
    return (values * columns[None, :]).astype(jnp.bfloat16)


def draw_output_matrix(key, part):
    random_subkeys = jax.random.split(jax.random.fold_in(key, 41), 2)
    features = spread(random_subkeys[0], D)
    values = table_entries(random_subkeys[1], (D, QUERY_HEADS * HEAD_DIM_SIZE)) * features[:, None] / math.sqrt(QUERY_HEADS * HEAD_DIM_SIZE)
    return values.astype(jnp.bfloat16)


def draw_down_matrix(key, part):
    random_subkeys = jax.random.split(jax.random.fold_in(key, 51), 2)
    features = spread(random_subkeys[0], D)
    values = table_entries(random_subkeys[1], (FF, D)) * features[None, :] / math.sqrt(FF)
    return values.astype(jnp.bfloat16)


def query_draws(key):
    random_subkeys = jax.random.split(jax.random.fold_in(key, 31), 2)
    softmax_weight = 0.5
    query_vectors = table_entries(random_subkeys[0], (BEAM_ROW_COUNT, QUERY_HEADS * HEAD_DIM_SIZE))
    weighted_total = query_vectors.reshape(BEAM_ROW_COUNT, KEY_VALUE_HEADS, QUERY_HEADS // KEY_VALUE_HEADS, HEAD_DIM_SIZE).sum(axis=2)
    gathered_keys = softmax_weight * weighted_total + 0.5 * table_entries(random_subkeys[1], (BEAM_ROW_COUNT, KEY_VALUE_HEADS, HEAD_DIM_SIZE))
    return (query_vectors, gathered_keys.reshape(BEAM_ROW_COUNT, KEY_VALUE_HEADS * HEAD_DIM_SIZE))


def draw_queries(key, part):
    return query_draws(key)[0].astype(jnp.bfloat16)


def draw_fresh_token_keys(key, part):
    return query_draws(key)[1].astype(jnp.bfloat16)


def page_plan(key):
    random_subkeys = jax.random.split(jax.random.fold_in(key, 7), 5)
    longest = TABLE_BLOCKS * PAGE_TOKENS - 1
    lengths = jax.random.randint(random_subkeys[0], (PROMPTS,), 1, longest + 1)
    long_one = jax.random.randint(random_subkeys[1], (), 0, PROMPTS)
    short_one = (long_one + 1 + jax.random.randint(random_subkeys[2], (), 0, PROMPTS - 1)) % PROMPTS
    prompt_index = jnp.arange(PROMPTS, dtype=jnp.int32)
    lengths = jnp.where(prompt_index == long_one, longest, jnp.where(prompt_index == short_one, 1, lengths))
    stride = TABLE_BLOCKS - 1 + BEAMS
    page_order = jax.random.permutation(random_subkeys[3], PAGE_SLOTS).astype(jnp.int32)
    chosen = jax.random.randint(random_subkeys[4], (), 0, PROMPTS * BEAMS)
    target = chosen // BEAMS * stride + TABLE_BLOCKS - 1 + chosen % BEAMS
    top_spot = jnp.sum(jnp.where(page_order == PAGE_SLOTS - 1, jnp.arange(PAGE_SLOTS, dtype=jnp.int32), 0))
    page_order = page_order.at[top_spot].set(page_order[target]).at[target].set(PAGE_SLOTS - 1)
    row_index = jnp.arange(BEAM_ROW_COUNT, dtype=jnp.int32)
    prompt_of = row_index // BEAMS
    beam_of = row_index % BEAMS
    column = jnp.arange(TABLE_BLOCKS, dtype=jnp.int32)[None, :]
    blocks = ((lengths + PAGE_TOKENS - 1) // PAGE_TOKENS)[prompt_of][:, None]
    shared_at = prompt_of[:, None] * stride + column
    own_at = prompt_of[:, None] * stride + TABLE_BLOCKS - 1 + beam_of[:, None]
    tables = jnp.where(column < blocks - 1, page_order[shared_at], jnp.where(column == blocks - 1, page_order[own_at], -1))
    return (lengths.astype(jnp.int32), tables.astype(jnp.int32))


def draw_prompt_lengths(key, part):
    return page_plan(key)[0]


def draw_block_tables(key, part):
    return page_plan(key)[1]


def draw_parents(key, part):
    row_index = jnp.arange(BEAM_ROW_COUNT, dtype=jnp.int32)
    picks = jax.random.randint(jax.random.fold_in(key, 11), (BEAM_ROW_COUNT,), 0, BEAMS)
    picks = picks.at[0].set(0).at[BEAM_ROW_COUNT - 1].set(BEAMS - 1)
    return (row_index // BEAMS * BEAMS + picks).astype(jnp.int32)


def block_scale(rng, extent, cuts, smallest, largest):
    gain, own = 1.0, jax.random.fold_in(rng, 6)
    for position, shards_of in cuts:
        steps = jnp.exp(jax.random.uniform(jax.random.fold_in(own, position), (shards_of,), jnp.float32, smallest / len(cuts), largest / len(cuts)))
        gain = gain * jnp.repeat(steps, extent[position] // shards_of).reshape([-1 if axis == position else 1 for axis in range(len(extent))])
    return gain


def gaussian(rng, shape, deviation, most, cuts=(), held_as=jnp.bfloat16):
    loudness = block_scale(rng, shape, cuts, -0.22, 0.18) if cuts else 1.0
    values = jax.random.normal(rng, shape, jnp.float32) * deviation * loudness
    return jnp.minimum(jnp.maximum(values, -most), most).astype(held_as)


def setup_inputs(seed: int = 0) -> dict:
    seeds = jax.random.split(jax.random.key(seed), 17)
    return {
        "queries": draw_queries(jax.random.fold_in(seeds[16], 71), 0),
        "fresh_token_keys": draw_fresh_token_keys(jax.random.fold_in(seeds[16], 71), 0),
        "fresh_token_values": gaussian(seeds[2], (BEAM_ROW_COUNT, KEY_VALUE_HEADS * HEAD_DIM_SIZE), 1.0, 6.0, ((0, 32), (1, 8))),
        "paged_keys": gaussian(seeds[3], (PAGE_SLOTS, PAGE_TOKENS, KEY_VALUE_HEADS * HEAD_DIM_SIZE), 1.0, 6.0, ((0, 32), (2, 8))),
        "paged_values": gaussian(seeds[4], (PAGE_SLOTS, PAGE_TOKENS, KEY_VALUE_HEADS * HEAD_DIM_SIZE), 1.0, 6.0, ((0, 32), (2, 8))),
        "block_tables": draw_block_tables(jax.random.fold_in(seeds[16], 71), 0),
        "parents": draw_parents(jax.random.fold_in(seeds[16], 71), 0),
        "prompt_lengths": draw_prompt_lengths(jax.random.fold_in(seeds[16], 71), 0),
        "stream": draw_stream(jax.random.fold_in(seeds[16], 71), 0),
        "output_matrix": draw_output_matrix(jax.random.fold_in(seeds[16], 71), 0),
        "attention_gain": jnp.clip(1.0 + 0.1 * jax.random.normal(seeds[10], (D,), jnp.float32), 0.5, 1.5).astype(jnp.bfloat16),
        "feedforward_gain": jnp.clip(1.0 + 0.1 * jax.random.normal(seeds[11], (D,), jnp.float32), 0.5, 1.5).astype(jnp.bfloat16),
        "gate_matrix": gaussian(seeds[12], (FF, D), D ** -0.5, 0.09375, ((0, 256),)),
        "linear_matrix": gaussian(seeds[13], (FF, D), D ** -0.5, 0.09375, ((0, 256),)),
        "down_matrix": draw_down_matrix(jax.random.fold_in(seeds[16], 71), 0),
        "closing_gain": jnp.clip(1.0 + 0.1 * jax.random.normal(seeds[15], (D,), jnp.float32), 0.5, 1.5).astype(jnp.bfloat16),
    }


norm_eps = 1e-06

def capped(scores):
    return SOFTCAP * jnp.tanh(scores / SOFTCAP)

def normalize(values, gain_row):
    mean_square = lax.optimization_barrier(jnp.mean(values * values, axis=1, keepdims=True))
    return values * lax.rsqrt(mean_square + norm_eps) * gain_row.astype(jnp.float32)[None, :]

def reference(queries, fresh_token_keys, fresh_token_values, paged_keys, paged_values, block_tables, parents, prompt_lengths, stream, output_matrix, attention_gain, feedforward_gain, gate_matrix, linear_matrix, down_matrix, closing_gain):
    query_groups = QUERY_HEADS // KEY_VALUE_HEADS
    root_scale = math.sqrt(QSCALAR)
    row_tables = jnp.take(block_tables, parents, axis=0)
    positions = jnp.arange(TABLE_BLOCKS * PAGE_TOKENS, dtype=jnp.int32)

    def one_row(current_row):
        fetched_pages = jnp.maximum(row_tables[current_row], 0)
        keys_of_row = jnp.take(paged_keys, fetched_pages, axis=0).reshape(TABLE_BLOCKS * PAGE_TOKENS, KEY_VALUE_HEADS, HEAD_DIM_SIZE).astype(jnp.float32)
        values_of_row = jnp.take(paged_values, fetched_pages, axis=0).reshape(TABLE_BLOCKS * PAGE_TOKENS, KEY_VALUE_HEADS, HEAD_DIM_SIZE).astype(jnp.float32)
        query_of_row = queries[current_row].reshape(KEY_VALUE_HEADS, query_groups, HEAD_DIM_SIZE).astype(jnp.float32)
        current_key = fresh_token_keys[current_row].reshape(KEY_VALUE_HEADS, HEAD_DIM_SIZE).astype(jnp.float32)
        current_value = fresh_token_values[current_row].reshape(KEY_VALUE_HEADS, HEAD_DIM_SIZE).astype(jnp.float32)
        limit = prompt_lengths[current_row // BEAMS]
        scores = capped(jnp.einsum('kgd,tkd->kgt', query_of_row, keys_of_row, precision=lax.Precision.HIGHEST) / root_scale)
        weights = jnp.where((positions < limit)[None, None, :], jnp.exp(scores), jnp.float32(0.0))
        self_weight = jnp.exp(capped(jnp.einsum('kgd,kd->kg', query_of_row, current_key, precision=lax.Precision.HIGHEST) / root_scale))
        totals = lax.optimization_barrier(jnp.sum(weights, axis=2)) + self_weight
        rounded = lax.optimization_barrier(weights.astype(jnp.bfloat16)).astype(jnp.float32)
        self_rounded = lax.optimization_barrier(self_weight.astype(jnp.bfloat16)).astype(jnp.float32)
        numerators = jnp.einsum('kgt,tkd->kgd', rounded, values_of_row, precision=lax.Precision.HIGHEST)
        numerators = numerators + self_rounded[:, :, None] * current_value[:, None, :]
        return (numerators / totals[:, :, None]).reshape(QUERY_HEADS * HEAD_DIM_SIZE).astype(jnp.bfloat16)
    attention = lax.map(one_row, jnp.arange(BEAM_ROW_COUNT, dtype=jnp.int32))
    projected = jnp.dot(attention, output_matrix.T, preferred_element_type=jnp.float32)
    residual = stream.astype(jnp.float32) + normalize(projected, attention_gain)
    normed = normalize(residual, feedforward_gain).astype(jnp.bfloat16)
    gate_sums = jnp.dot(normed, gate_matrix.T, preferred_element_type=jnp.float32)
    lift_sums = jnp.dot(normed, linear_matrix.T, preferred_element_type=jnp.float32)
    hidden = (jax.nn.gelu(gate_sums, approximate=True) * lift_sums).astype(jnp.bfloat16)
    feedforward = jnp.dot(hidden, down_matrix, preferred_element_type=jnp.float32)
    return (residual + normalize(feedforward, closing_gain)).astype(jnp.bfloat16)
```

```python
import math

import jax
import jax.numpy as jnp
from jax import lax
from jax.sharding import Mesh, PartitionSpec as P

HEAD_DIM_SIZE = 128
QSCALAR = 144
SOFTCAP = 50
BEAMS = 8
Z, X, Y, C = 8, 4, 4, 2
PAGES = Z * X


norm_eps = 1e-06


def capped(scores):
    return SOFTCAP * jnp.tanh(scores / SOFTCAP)


def normalize(values, gain_row):
    mean_square = jnp.mean(values * values, axis=1, keepdims=True)
    return values * lax.rsqrt(mean_square + norm_eps) * gain_row.astype(jnp.float32)[None, :]


def exchange(blocks, axes):
    return lax.all_to_all(blocks, axes, 0, 0, tiled=True)


def gather_blocks(block, axes, count):
    return exchange(jnp.broadcast_to(block[None], (count,) + block.shape), axes)


def per_device(
    queries,
    fresh_token_keys,
    fresh_token_values,
    paged_keys,
    paged_values,
    block_tables,
    parents,
    prompt_lengths,
    stream,
    output_matrix,
    attention_gain,
    feedforward_gain,
    gate_matrix,
    linear_matrix,
    down_matrix,
    closing_gain,
):
    swap = [(0, 1), (1, 0)]
    gate_other = lax.ppermute(gate_matrix, "c", swap)
    linear_other = lax.ppermute(linear_matrix, "c", swap)
    down_other = lax.ppermute(down_matrix, "c", swap)

    home_rows = queries.shape[0]
    slot_count = paged_keys.shape[0]
    page_len = paged_keys.shape[1]
    kv_heads = paged_keys.shape[2] // HEAD_DIM_SIZE
    query_groups = queries.shape[1] // HEAD_DIM_SIZE // kv_heads
    root_scale = math.sqrt(QSCALAR)
    page_id = lax.axis_index("z") * X + lax.axis_index("x")
    all_queries = gather_blocks(queries, ("z", "x"), PAGES).reshape(-1, queries.shape[1])
    row_count = all_queries.shape[0]
    row_tables = jnp.take(block_tables, parents, axis=0)
    slot_ids = page_id * slot_count + jnp.arange(slot_count, dtype=jnp.int32)
    matches = row_tables[None, :, :] == slot_ids[:, None, None]
    in_use = jnp.any(matches, axis=2)
    block_index = jnp.arange(row_tables.shape[1], dtype=jnp.int32)
    block_pos = jnp.sum(jnp.where(matches, block_index[None, None, :], 0), axis=2)
    row_ids = jnp.arange(row_count, dtype=jnp.int32)
    owner_prompt = jnp.max(jnp.where(in_use, (row_ids // BEAMS)[None, :], -1), axis=1)
    prompt_ids = jnp.maximum(owner_prompt, 0)
    beam_rows = prompt_ids[:, None] * BEAMS + jnp.arange(BEAMS, dtype=jnp.int32)[None, :]
    row_in_use = jnp.take_along_axis(in_use, beam_rows, axis=1)
    row_block = jnp.take_along_axis(block_pos, beam_rows, axis=1)
    limits = jnp.take(prompt_lengths, prompt_ids)
    positions = (
        row_block[:, :, None] * page_len + jnp.arange(page_len, dtype=jnp.int32)[None, None, :]
    )
    visible = jnp.logical_and(row_in_use[:, :, None], positions < limits[:, None, None])
    slot_queries = jnp.take(all_queries, beam_rows.reshape(-1), axis=0).reshape(
        slot_count, BEAMS, kv_heads, query_groups, HEAD_DIM_SIZE
    )
    page_keys = paged_keys.reshape(slot_count, page_len, kv_heads, HEAD_DIM_SIZE)
    page_values = paged_values.reshape(slot_count, page_len, kv_heads, HEAD_DIM_SIZE)
    raw_scores = jnp.einsum(
        "sbkgd,stkd->sbkgt", slot_queries, page_keys, preferred_element_type=jnp.float32
    )
    weights = jnp.where(
        visible[:, :, None, None, :], jnp.exp(capped(raw_scores / root_scale)), jnp.float32(0.0)
    )
    slot_totals = jnp.sum(weights, axis=4)
    slot_numerators = jnp.einsum(
        "sbkgt,stkd->sbkgd",
        weights.astype(jnp.bfloat16),
        page_values,
        preferred_element_type=jnp.float32,
    )
    selector = (beam_rows[:, :, None] == row_ids[None, None, :]).astype(jnp.float32)
    payload = jnp.concatenate(
        [
            slot_numerators.reshape(slot_count, BEAMS, -1),
            slot_totals.reshape(slot_count, BEAMS, -1),
        ],
        axis=2,
    )
    rows_out = jnp.einsum("avz,avo->zo", selector, payload, precision=lax.Precision.HIGHEST)
    width = queries.shape[1]
    tops = rows_out[:, width:]
    high = tops.astype(jnp.bfloat16)
    low = (tops - high.astype(jnp.float32)).astype(jnp.bfloat16)
    sent = jnp.concatenate(
        [rows_out[:, :width].astype(jnp.bfloat16), high, low, jnp.zeros((row_count, 120), jnp.bfloat16)],
        axis=1,
    )
    got = exchange(sent.reshape(PAGES, home_rows, width + 128), ("z", "x"))
    summed = jnp.sum(got.astype(jnp.float32), axis=0)
    home_numerators = summed[:, :width]
    home_totals = summed[:, width : width + 4] + summed[:, width + 4 : width + 8]
    own_queries = queries.reshape(home_rows, kv_heads, query_groups, HEAD_DIM_SIZE)
    own_keys = fresh_token_keys.reshape(home_rows, kv_heads, HEAD_DIM_SIZE)
    own_values = fresh_token_values.reshape(home_rows, kv_heads, HEAD_DIM_SIZE)
    self_weight = jnp.exp(
        capped(
            jnp.einsum("rkgd,rkd->rkg", own_queries, own_keys, preferred_element_type=jnp.float32)
            / root_scale
        )
    )
    totals = home_totals.reshape(home_rows, kv_heads, query_groups) + self_weight
    self_term = jnp.einsum(
        "rkg,rkd->rkgd",
        self_weight.astype(jnp.bfloat16),
        own_values,
        preferred_element_type=jnp.float32,
    )
    numerators = (
        home_numerators.reshape(home_rows, kv_heads, query_groups, HEAD_DIM_SIZE) + self_term
    )
    attention = (numerators / totals[:, :, :, None]).reshape(home_rows, -1).astype(jnp.bfloat16)
    head_terms = lax.dot_general(
        attention, output_matrix, (((1,), (1,)), ((), ())), preferred_element_type=jnp.float32
    ).astype(jnp.bfloat16)
    projected = jnp.sum(
        exchange(head_terms, ("y", "c")).astype(jnp.float32), axis=0, keepdims=True
    )
    residual = stream.astype(jnp.float32) + normalize(projected, attention_gain)
    normed = normalize(residual, feedforward_gain).astype(jnp.bfloat16)
    over_z = exchange(jnp.broadcast_to(normed, (Z, normed.shape[1])), "z")
    segment = gather_blocks(over_z, ("x", "y"), X * Y).reshape(X * Y * Z, -1)

    def dot_t(a, b):
        return lax.dot_general(a, b, (((1,), (1,)), ((), ())), preferred_element_type=jnp.float32)

    def part(gate, linear, down):
        hidden = jax.nn.gelu(dot_t(segment, gate), approximate=True) * dot_t(segment, linear)
        return jnp.dot(hidden.astype(jnp.bfloat16), down, preferred_element_type=jnp.float32)

    terms = part(gate_matrix, linear_matrix, down_matrix) + part(
        gate_other, linear_other, down_other
    )
    sent = terms.astype(jnp.bfloat16).reshape(X * Y, Z, -1)
    over_xy = jnp.sum(exchange(sent, ("x", "y")).astype(jnp.float32), axis=0)
    feedforward = jnp.sum(
        exchange(over_xy.astype(jnp.bfloat16), "z").astype(jnp.float32), axis=0, keepdims=True
    )
    return (residual + normalize(feedforward, closing_gain)).astype(jnp.bfloat16)


def solution(mesh):
    torus = Mesh(mesh.devices.reshape(Z, X, Y, C), ("z", "x", "y", "c"))
    page, feat, both = ("z", "x"), ("y", "c"), ("z", "x", "y", "c")
    placed = (
        P(page, feat),
        P(page, feat),
        P(page, feat),
        P(page, None, feat),
        P(page, None, feat),
        P(),
        P(),
        P(),
        P(both, None),
        P(None, feat),
        P(),
        P(),
        P(both, None),
        P(both, None),
        P(both, None),
        P(),
    )
    return jax.shard_map(
        per_device, mesh=torus, in_specs=placed, out_specs=P(both, None), check_vma=False
    )
```

```python
import jax
import jax.numpy as jnp
from jax import lax
from jax.experimental import pallas as pl
from jax.experimental.pallas import tpu as pltpu
from jax.sharding import Mesh, PartitionSpec as P

HEAD = 128
ROOT_SCALE = 12.0
SOFTCAP = 50.0
BEAMS = 8
Z, X, Y, C = 8, 4, 4, 2
PAGES = Z * X
D = 4608
FOLD = 640
SLOTS = 16
PAGE = 256
BF, F32 = jnp.bfloat16, jnp.float32

norm_eps = 1e-06


def kernel(body, outs, scratch=(), smem=0, n_in=0):
    specs = [pl.BlockSpec(memory_space=pltpu.SMEM)] * smem
    specs += [pl.BlockSpec(memory_space=pltpu.VMEM)] * (n_in - smem)
    return pl.pallas_call(
        body,
        out_shape=outs,
        in_specs=specs,
        out_specs=jax.tree.map(lambda _: pl.BlockSpec(memory_space=pltpu.VMEM), outs),
        scratch_shapes=list(scratch),
        name=body.__name__,
    )


def weight_of(raw):
    return jnp.exp(SOFTCAP * jnp.tanh(raw * (1.0 / (ROOT_SCALE * SOFTCAP))))


def dot_nt(a, b):
    return lax.dot_general(a, b, (((1,), (1,)), ((), ())), preferred_element_type=F32)


def attend(prompt, valid, q, k, v, out, acc, tacc):
    acc[...] = jnp.zeros_like(acc)
    tacc[...] = jnp.zeros_like(tacc)
    token = lax.broadcasted_iota(jnp.int32, (BEAMS, PAGE), 1)
    lane = lax.broadcasted_iota(jnp.int32, (BEAMS, HEAD), 1)
    for s in range(SLOTS):
        p = prompt[s]
        queries = q[p].astype(F32)
        live = token < valid[:, s : s + 1]
        live = jnp.concatenate([live, live], axis=0)
        sums = jnp.zeros((BEAMS, HEAD), F32)
        nums = []
        for h in range(2):
            pair = jnp.concatenate(
                [queries[:, (2 * h + g) * HEAD : (2 * h + g + 1) * HEAD] for g in range(2)], axis=0
            ).astype(BF)
            w = weight_of(dot_nt(pair, k[s, :, h * HEAD : (h + 1) * HEAD]))
            w = jnp.where(live, w, 0.0)
            t = jnp.sum(w, axis=1, keepdims=True)
            n = jnp.dot(w.astype(BF), v[s, :, h * HEAD : (h + 1) * HEAD], preferred_element_type=F32)
            for g in range(2):
                sums = jnp.where(lane % 4 == 2 * h + g, t[g * BEAMS : (g + 1) * BEAMS], sums)
                nums.append(n[g * BEAMS : (g + 1) * BEAMS])
        acc[p] += jnp.concatenate(nums, axis=1)
        tacc[p] += sums
    out[:, :, : 4 * HEAD] = acc[...].astype(BF)
    t = tacc[...]
    high = t.astype(BF).astype(F32)
    upper = lax.broadcasted_iota(jnp.int32, t.shape, 2) < 4
    out[:, :, 4 * HEAD :] = jnp.where(upper, high, t - high).astype(BF)


def fold_rows(parts, out, rows):
    for a in range(8):
        part = parts(a)
        for b in range(5):
            rows[pl.ds(64 * b + a, 8, stride=8), :] = part[:, b * HEAD : (b + 1) * HEAD]
    for r in range(8):
        for b in range(5):
            low = 64 * b + 8 * r
            out[r, :, b * HEAD : (b + 1) * HEAD] = rows[low : low + 8, :].astype(BF)


def project(got, q, fresh_k, fresh_v, wo, out, rows):
    total = got[0].astype(F32)
    for i in range(1, PAGES):
        total += got[i].astype(F32)
    heads = []
    for h in range(4):
        k = h // 2
        hs, ks = slice(h * HEAD, (h + 1) * HEAD), slice(k * HEAD, (k + 1) * HEAD)
        raw = jnp.sum(q[:, hs].astype(F32) * fresh_k[:, ks].astype(F32), axis=1, keepdims=True)
        own = weight_of(raw)
        base = 4 * HEAD + h
        denominator = total[:, base : base + 1] + total[:, base + 4 : base + 5] + own
        numerator = total[:, hs] + own.astype(BF).astype(F32) * fresh_v[:, ks].astype(F32)
        heads.append(numerator / denominator)
    attention = jnp.concatenate(heads, axis=1).astype(BF)

    def part(a):
        lo, hi = a * FOLD, min(D, (a + 1) * FOLD)
        terms = dot_nt(attention, wo[lo:hi, :])
        if hi - lo < FOLD:
            terms = jnp.concatenate([terms, jnp.zeros((8, FOLD - hi + lo), F32)], axis=1)
        return terms

    fold_rows(part, out, rows)


def total_of(got, count):
    total = got[0].astype(F32)
    for i in range(1, count):
        total += got[i].astype(F32)
    return total


def unit(v):
    square = jnp.sum(jnp.sum(v * v, axis=1, keepdims=True), axis=0, keepdims=True)
    return v * lax.rsqrt(square * (1.0 / D) + norm_eps)


def enter(got, stream, gain_a, gain_f, residual, spread):
    r = stream[...].astype(F32) + unit(total_of(got, Y * C)) * gain_a[...].astype(F32)
    residual[...] = r
    normed = (unit(r) * gain_f[...].astype(F32)).astype(BF)
    for i in range(Z):
        spread[i] = normed


def widen(got, out, rows):
    for z in range(Z):
        for b in range(5):
            low = 64 * b + 8 * z
            rows[low : low + 8, :] = got[z, :, b * HEAD : (b + 1) * HEAD].astype(F32)
    for t in range(D // HEAD):
        part = rows[pl.ds(64 * (t % 5) + t // 5, 8, stride=8), :].astype(BF)
        for i in range(X * Y):
            out[i, :, t * HEAD : (t + 1) * HEAD] = part


def feed(x, g0, l0, g1, l1, d0, d1, out):
    rows = x[...]

    def hidden(g, l):
        gate = dot_nt(rows, g[...])
        return (jax.nn.gelu(gate, approximate=True) * dot_nt(rows, l[...])).astype(BF)

    h0, h1 = hidden(g0, l0), hidden(g1, l1)
    step = 512
    for c in range(0, D, step):
        cut = slice(c, c + step)
        y = jnp.dot(h0, d0[:, cut], preferred_element_type=F32)
        y += jnp.dot(h1, d1[:, cut], preferred_element_type=F32)
        out[:, cut] = y.astype(BF)


def gather_sum(got, out, rows):
    def part(a):
        lo, hi = a * FOLD, min(D, (a + 1) * FOLD)
        total = got[0, :, lo:hi].astype(F32)
        for i in range(1, X * Y):
            total += got[i, :, lo:hi].astype(F32)
        if hi - lo < FOLD:
            total = jnp.concatenate([total, jnp.zeros((8, FOLD - hi + lo), F32)], axis=1)
        return total

    fold_rows(part, out, rows)


def leave(got, residual, gain, out):
    value = residual[...] + unit(total_of(got, Z)) * gain[...].astype(F32)
    for a in range(8):
        lo, hi = a * FOLD, min(D, (a + 1) * FOLD)
        out[:, lo:hi] = value[a : a + 1, : hi - lo].astype(BF)


def exchange(blocks, axes):
    return lax.all_to_all(blocks, axes, 0, 0, tiled=True)


def fold(v):
    return jnp.pad(v.reshape(-1), (0, 8 * FOLD - D)).reshape(8, FOLD)


def shaped(*shape, dtype=BF):
    return jax.ShapeDtypeStruct(shape, dtype)


def per_device(
    queries,
    fresh_token_keys,
    fresh_token_values,
    paged_keys,
    paged_values,
    block_tables,
    parents,
    prompt_lengths,
    stream,
    output_matrix,
    attention_gain,
    feedforward_gain,
    gate_matrix,
    linear_matrix,
    down_matrix,
    closing_gain,
):
    swap = [(0, 1), (1, 0)]
    gate_other = lax.ppermute(gate_matrix, "c", swap)
    linear_other = lax.ppermute(linear_matrix, "c", swap)
    down_other = lax.ppermute(down_matrix, "c", swap)

    all_queries = exchange(jnp.broadcast_to(queries[None], (PAGES,) + queries.shape), ("z", "x"))
    page_id = lax.axis_index("z") * X + lax.axis_index("x")
    slots = page_id * SLOTS + jnp.arange(SLOTS, dtype=jnp.int32)
    row_ids = jnp.arange(block_tables.shape[0], dtype=jnp.int32)
    lengths = jnp.repeat(prompt_lengths, BEAMS)
    first = PAGE * jnp.arange(block_tables.shape[1], dtype=jnp.int32)
    tokens = jnp.clip(lengths[:, None] - first[None, :], 0, PAGE)
    held = jnp.sum(
        jnp.where(block_tables[None] == slots[:, None, None], tokens[None], 0), axis=2
    )
    prompt = jnp.max(jnp.where(held > 0, (row_ids // BEAMS)[None], 0), axis=1)
    chosen = jnp.repeat(parents.reshape(-1, BEAMS), BEAMS, axis=0) == row_ids[:, None]
    valid = jnp.sum(jnp.where(chosen.T[:, None, :], held[None], 0), axis=2)

    sent = kernel(
        attend,
        shaped(PAGES, BEAMS, 5 * HEAD),
        [pltpu.VMEM((PAGES, BEAMS, 4 * HEAD), F32), pltpu.VMEM((PAGES, BEAMS, HEAD), F32)],
        1,
        5,
    )(prompt, valid, all_queries, paged_keys, paged_values)
    got = exchange(sent, ("z", "x"))
    rows = [pltpu.VMEM((5 * 64, HEAD), F32)]
    blocks = shaped(8, 8, FOLD)
    sent = kernel(project, blocks, rows, 0, 5)(
        got, queries, fresh_token_keys, fresh_token_values, output_matrix
    )
    got = exchange(sent, ("y", "c"))
    residual, sent = kernel(enter, (shaped(8, FOLD, dtype=F32), blocks), (), 0, 4)(
        got, fold(stream), fold(attention_gain), fold(feedforward_gain)
    )
    got = exchange(sent, "z")
    sent = kernel(widen, shaped(X * Y, Z, D), rows, 0, 1)(got)
    got = exchange(sent, ("x", "y")).reshape(X * Y * Z, D)
    sent = kernel(feed, shaped(X * Y * Z, D), (), 0, 7)(
        got, gate_matrix, linear_matrix, gate_other, linear_other, down_matrix, down_other
    )
    got = exchange(sent.reshape(X * Y, Z, D), ("x", "y"))
    sent = kernel(gather_sum, blocks, rows, 0, 1)(got)
    got = exchange(sent, "z")
    return kernel(leave, shaped(1, D), (), 0, 3)(got, residual, fold(closing_gain))


def solution(mesh):
    torus = Mesh(mesh.devices.reshape(Z, X, Y, C), ("z", "x", "y", "c"))
    page, feat, both = ("z", "x"), ("y", "c"), ("z", "x", "y", "c")
    placed = (
        P(page, feat),
        P(page, feat),
        P(page, feat),
        P(page, None, feat),
        P(page, None, feat),
        P(),
        P(),
        P(),
        P(both, None),
        P(None, feat),
        P(),
        P(),
        P(both, None),
        P(both, None),
        P(both, None),
        P(),
    )
    return jax.shard_map(
        per_device, mesh=torus, in_specs=placed, out_specs=P(both, None), check_vma=False
    )
```

```python
import jax
import jax.numpy as jnp
from jax import lax
from jax.experimental import pallas as pl
from jax.experimental.pallas import tpu as pltpu
from jax.sharding import Mesh, PartitionSpec as P

HEAD = 128
ROOT_SCALE = 12.0
SOFTCAP = 50.0
BEAMS = 8
Z, X, Y, C = 8, 4, 4, 2
PAGES = Z * X
D = 4608
FOLD = 640
SLOTS = 16
PAGE = 256
BATCH = 4
BF, F32 = jnp.bfloat16, jnp.float32
VMEM, SMEM, HBM = pltpu.VMEM, pltpu.SMEM, pltpu.HBM

norm_eps = 1e-06


def kernel(body, outs, spaces, scratch=(), mib=4):
    return pl.pallas_call(
        body,
        out_shape=outs,
        in_specs=[pl.BlockSpec(memory_space=m) for m in spaces],
        out_specs=jax.tree.map(lambda _: pl.BlockSpec(memory_space=VMEM), outs),
        scratch_shapes=list(scratch),
        name=body.__name__,
        compiler_params=pltpu.CompilerParams(vmem_limit_bytes=mib << 20),
    )


def weight_of(raw):
    return jnp.exp(SOFTCAP * jnp.tanh(raw * (1.0 / (ROOT_SCALE * SOFTCAP))))


def dot_nt(a, b):
    return lax.dot_general(a, b, (((1,), (1,)), ((), ())), preferred_element_type=F32)


def attend(prompt, valid, q, k_hbm, v_hbm, out, k, v, acc, tacc, k_sem, v_sem):
    def fetch(n, hbm, buf, sem):
        some = pl.ds(n * BATCH, BATCH)
        return pltpu.make_async_copy(hbm.at[some], buf.at[some], sem.at[n])

    for n in range(SLOTS // BATCH):
        fetch(n, k_hbm, k, k_sem).start()
        fetch(n, v_hbm, v, v_sem).start()
    acc[...] = jnp.zeros_like(acc)
    tacc[...] = jnp.zeros_like(tacc)
    token = lax.broadcasted_iota(jnp.int32, (BEAMS, PAGE), 1)
    lane = lax.broadcasted_iota(jnp.int32, (BEAMS, HEAD), 1) % 4
    blank = jnp.zeros((2 * BEAMS, HEAD), F32)
    for n in range(SLOTS // BATCH):
        slots = range(n * BATCH, (n + 1) * BATCH)
        fetch(n, k_hbm, k, k_sem).wait()
        scores, live = [], []
        for s in slots:
            queries = q[prompt[s]].astype(F32)
            heads = [queries[:, i * HEAD : (i + 1) * HEAD] for i in range(4)]
            left = jnp.concatenate([heads[0], heads[1], blank], axis=0)
            right = jnp.concatenate([blank, heads[2], heads[3]], axis=0)
            scores.append(dot_nt(jnp.concatenate([left, right], axis=1).astype(BF), k[s]))
            live += [token < valid[:, s : s + 1]] * 4
        w = weight_of(jnp.concatenate(scores, axis=0))
        w = jnp.where(jnp.concatenate(live, axis=0), w, 0.0)
        t = jnp.sum(w, axis=1, keepdims=True)
        wb = w.astype(BF)
        fetch(n, v_hbm, v, v_sem).wait()
        for i, s in enumerate(slots):
            p = prompt[s]
            m = jnp.dot(wb[32 * i : 32 * i + 32], v[s], preferred_element_type=F32)
            acc[p] += jnp.concatenate(
                [m[0:8, :HEAD], m[8:16, :HEAD], m[16:24, HEAD:], m[24:32, HEAD:]], axis=1
            )
            sums = jnp.zeros((BEAMS, HEAD), F32)
            for j in range(4):
                sums = jnp.where(lane == j, t[32 * i + 8 * j : 32 * i + 8 * j + 8], sums)
            tacc[p] += sums
    out[:, :, : 4 * HEAD] = acc[...].astype(BF)
    t = tacc[...]
    high = t.astype(BF).astype(F32)
    upper = lax.broadcasted_iota(jnp.int32, t.shape, 2) < 4
    out[:, :, 4 * HEAD :] = jnp.where(upper, high, t - high).astype(BF)


def fold_rows(parts, out, rows):
    for a in range(8):
        part = parts(a)
        for b in range(5):
            rows[pl.ds(64 * b + a, 8, stride=8), :] = part[:, b * HEAD : (b + 1) * HEAD]
    for r in range(8):
        for b in range(5):
            low = 64 * b + 8 * r
            out[r, :, b * HEAD : (b + 1) * HEAD] = rows[low : low + 8, :].astype(BF)


def project(got, q, fresh_k, fresh_v, wo, out, rows):
    total = got[0].astype(F32)
    for i in range(1, PAGES):
        total += got[i].astype(F32)
    heads = []
    for h in range(4):
        k = h // 2
        hs, ks = slice(h * HEAD, (h + 1) * HEAD), slice(k * HEAD, (k + 1) * HEAD)
        raw = jnp.sum(q[:, hs].astype(F32) * fresh_k[:, ks].astype(F32), axis=1, keepdims=True)
        own = weight_of(raw)
        base = 4 * HEAD + h
        denominator = total[:, base : base + 1] + total[:, base + 4 : base + 5] + own
        numerator = total[:, hs] + own.astype(BF).astype(F32) * fresh_v[:, ks].astype(F32)
        heads.append(numerator / denominator)
    attention = jnp.concatenate(heads, axis=1).astype(BF)

    def part(a):
        lo, hi = a * FOLD, min(D, (a + 1) * FOLD)
        terms = dot_nt(attention, wo[lo:hi, :])
        if hi - lo < FOLD:
            terms = jnp.concatenate([terms, jnp.zeros((8, FOLD - hi + lo), F32)], axis=1)
        return terms

    fold_rows(part, out, rows)


def total_of(got, count):
    total = got[0].astype(F32)
    for i in range(1, count):
        total += got[i].astype(F32)
    return total


def unit(v):
    square = jnp.sum(jnp.sum(v * v, axis=1, keepdims=True), axis=0, keepdims=True)
    return v * lax.rsqrt(square * (1.0 / D) + norm_eps)


def enter(got, vectors, residual, spread):
    r = vectors[0].astype(F32) + unit(total_of(got, Y * C)) * vectors[1].astype(F32)
    residual[...] = r
    normed = (unit(r) * vectors[2].astype(F32)).astype(BF)
    for i in range(Z):
        spread[i] = normed


def widen(got, out, rows):
    for z in range(Z):
        for b in range(5):
            low = 64 * b + 8 * z
            rows[low : low + 8, :] = got[z, :, b * HEAD : (b + 1) * HEAD].astype(F32)
    for t in range(D // HEAD):
        part = rows[pl.ds(64 * (t % 5) + t // 5, 8, stride=8), :].astype(BF)
        for i in range(X * Y):
            out[i, :, t * HEAD : (t + 1) * HEAD] = part


def feed(x, g0, l0, g1, l1, d0, d1_hbm, out, d1, sem):
    late = pltpu.make_async_copy(d1_hbm, d1, sem)
    late.start()
    rows = x[...]

    def hidden(g, l):
        gate = dot_nt(rows, g[...])
        return (jax.nn.gelu(gate, approximate=True) * dot_nt(rows, l[...])).astype(BF)

    h0, h1 = hidden(g0, l0), hidden(g1, l1)
    late.wait()
    step = 512
    for c in range(0, D, step):
        cut = slice(c, c + step)
        y = jnp.dot(h0, d0[:, cut], preferred_element_type=F32)
        y += jnp.dot(h1, d1[:, cut], preferred_element_type=F32)
        out[:, cut] = y.astype(BF)


def gather_sum(got, out, rows):
    def part(a):
        lo, hi = a * FOLD, min(D, (a + 1) * FOLD)
        total = got[0, :, lo:hi].astype(F32)
        for i in range(1, X * Y):
            total += got[i, :, lo:hi].astype(F32)
        if hi - lo < FOLD:
            total = jnp.concatenate([total, jnp.zeros((8, FOLD - hi + lo), F32)], axis=1)
        return total

    fold_rows(part, out, rows)


def leave(got, residual, vectors, out):
    value = residual[...] + unit(total_of(got, Z)) * vectors[3].astype(F32)
    for a in range(8):
        lo, hi = a * FOLD, min(D, (a + 1) * FOLD)
        out[:, lo:hi] = value[a : a + 1, : hi - lo].astype(BF)


def exchange(blocks, axes):
    return lax.all_to_all(blocks, axes, 0, 0, tiled=True)


def stay(v):
    return pltpu.with_memory_space_constraint(v, HBM)


def shaped(*shape, dtype=BF):
    return jax.ShapeDtypeStruct(shape, dtype)


def per_device(
    queries,
    fresh_token_keys,
    fresh_token_values,
    paged_keys,
    paged_values,
    block_tables,
    parents,
    prompt_lengths,
    stream,
    output_matrix,
    attention_gain,
    feedforward_gain,
    gate_matrix,
    linear_matrix,
    down_matrix,
    closing_gain,
):
    swap = [(0, 1), (1, 0)]
    gate_other = lax.ppermute(gate_matrix, "c", swap)
    linear_other = lax.ppermute(linear_matrix, "c", swap)
    down_other = lax.ppermute(down_matrix, "c", swap)

    all_queries = exchange(jnp.broadcast_to(queries[None], (PAGES,) + queries.shape), ("z", "x"))
    page_id = lax.axis_index("z") * X + lax.axis_index("x")
    slots = page_id * SLOTS + jnp.arange(SLOTS, dtype=jnp.int32)
    row_ids = jnp.arange(block_tables.shape[0], dtype=jnp.int32)
    lengths = jnp.repeat(prompt_lengths, BEAMS)
    first = PAGE * jnp.arange(block_tables.shape[1], dtype=jnp.int32)
    tokens = jnp.clip(lengths[:, None] - first[None, :], 0, PAGE)
    held = jnp.sum(
        jnp.where(block_tables[None] == slots[:, None, None], tokens[None], 0), axis=2
    )
    prompt = jnp.max(jnp.where(held > 0, (row_ids // BEAMS)[None], 0), axis=1)
    chosen = jnp.repeat(parents.reshape(-1, BEAMS), BEAMS, axis=0) == row_ids[:, None]
    valid = jnp.sum(jnp.where(chosen.T[:, None, :], held[None], 0), axis=2)

    vectors = jnp.stack([stream[0], attention_gain, feedforward_gain, closing_gain])
    vectors = jnp.pad(vectors, ((0, 0), (0, 8 * FOLD - D))).reshape(4, 8, FOLD)
    all_queries, vectors = lax.optimization_barrier((all_queries, vectors))

    pages = pltpu.VMEM(paged_keys.shape, BF)
    batches = pltpu.SemaphoreType.DMA((SLOTS // BATCH,))
    sent = kernel(
        attend,
        shaped(PAGES, BEAMS, 5 * HEAD),
        (SMEM, VMEM, VMEM, HBM, HBM),
        [
            pages,
            pages,
            pltpu.VMEM((PAGES, BEAMS, 4 * HEAD), F32),
            pltpu.VMEM((PAGES, BEAMS, HEAD), F32),
            batches,
            batches,
        ],
        8,
    )(prompt, valid, all_queries, stay(paged_keys), stay(paged_values))
    got = exchange(sent, ("z", "x"))
    rows = [pltpu.VMEM((5 * 64, HEAD), F32)]
    blocks = shaped(8, 8, FOLD)
    sent = kernel(
        project,
        blocks,
        (VMEM,) * 5,
        rows,
        8,
    )(got, queries, fresh_token_keys, fresh_token_values, output_matrix)
    sent, gate_other, linear_other, down_other = lax.optimization_barrier(
        (sent, gate_other, linear_other, down_other)
    )
    got = exchange(sent, ("y", "c"))
    residual, sent = kernel(enter, (shaped(8, FOLD, dtype=F32), blocks), (VMEM,) * 2)(got, vectors)
    got = exchange(sent, "z")
    sent = kernel(widen, shaped(X * Y, Z, D), (VMEM,), rows)(got)
    got = exchange(sent, ("x", "y")).reshape(X * Y * Z, D)
    late = [pltpu.VMEM(down_matrix.shape, BF), pltpu.SemaphoreType.DMA(())]
    sent = kernel(feed, shaped(X * Y * Z, D), (VMEM,) * 6 + (HBM,), late, 16)(
        got, gate_matrix, linear_matrix, gate_other, linear_other, down_matrix, down_other
    )
    got = exchange(sent.reshape(X * Y, Z, D), ("x", "y"))
    sent = kernel(gather_sum, blocks, (VMEM,), rows)(got)
    got = exchange(sent, "z")
    return kernel(leave, shaped(1, D), (VMEM,) * 3)(got, residual, vectors)


def solution(mesh):
    torus = Mesh(mesh.devices.reshape(Z, X, Y, C), ("z", "x", "y", "c"))
    page, feat, both = ("z", "x"), ("y", "c"), ("z", "x", "y", "c")
    placed = (
        P(page, feat),
        P(page, feat),
        P(page, feat),
        P(page, None, feat),
        P(page, None, feat),
        P(),
        P(),
        P(),
        P(both, None),
        P(None, feat),
        P(),
        P(),
        P(both, None),
        P(both, None),
        P(both, None),
        P(),
    )
    return jax.shard_map(
        per_device, mesh=torus, in_specs=placed, out_specs=P(both, None), check_vma=False
    )
```

```python
import jax
import jax.numpy as jnp
from jax import lax
from jax.experimental import pallas as pl
from jax.experimental.pallas import tpu as pltpu
from jax.sharding import Mesh, PartitionSpec as P

HEAD = 128
ROOT_SCALE = 12.0
SOFTCAP = 50.0
BEAMS = 8
Z, X, Y, C = 8, 4, 4, 2
PAGES = Z * X
D = 4608
TILES = D // HEAD
FOLD = 40
SLOTS = 16
PAGE = 256
BATCH = 8
BF, F32 = jnp.bfloat16, jnp.float32
VMEM, SMEM, HBM = pltpu.VMEM, pltpu.SMEM, pltpu.HBM

norm_eps = 1e-06


def kernel(body, outs, spaces, scratch=(), mib=4):
    return pl.pallas_call(
        body,
        out_shape=outs,
        in_specs=[pl.BlockSpec(memory_space=m) for m in spaces],
        out_specs=jax.tree.map(lambda _: pl.BlockSpec(memory_space=VMEM), outs),
        scratch_shapes=list(scratch),
        compiler_params=pltpu.CompilerParams(vmem_limit_bytes=mib << 20),
    )


def weight_of(raw):
    return jnp.exp(SOFTCAP * jnp.tanh(raw * (1.0 / (ROOT_SCALE * SOFTCAP))))


def dot_nt(a, b):
    return lax.dot_general(a, b, (((1,), (1,)), ((), ())), preferred_element_type=F32)


def attend(prompt, valid, q, k_hbm, v_hbm, out, k, v, acc, tacc, k_sem, v_sem):
    def fetch(n, hbm, buf, sem):
        some = pl.ds(n * BATCH, BATCH)
        return pltpu.make_async_copy(hbm.at[some], buf.at[some], sem.at[n])

    for n in range(SLOTS // BATCH):
        fetch(n, k_hbm, k, k_sem).start()
        fetch(n, v_hbm, v, v_sem).start()
    acc[...] = jnp.zeros_like(acc)
    tacc[...] = jnp.zeros_like(tacc)
    token = lax.broadcasted_iota(jnp.int32, (BEAMS, PAGE), 1)
    lane = lax.broadcasted_iota(jnp.int32, (BEAMS, HEAD), 1) % 4
    blank = jnp.zeros((2 * BEAMS, HEAD), F32)
    for n in range(SLOTS // BATCH):
        slots = range(n * BATCH, (n + 1) * BATCH)
        fetch(n, k_hbm, k, k_sem).wait()
        scores, live = [], []
        for s in slots:
            queries = q[prompt[s, 0]].astype(F32)
            heads = [queries[:, i * HEAD : (i + 1) * HEAD] for i in range(4)]
            left = jnp.concatenate([heads[0], heads[1], blank], axis=0)
            right = jnp.concatenate([blank, heads[2], heads[3]], axis=0)
            scores.append(dot_nt(jnp.concatenate([left, right], axis=1).astype(BF), k[s]))
            live += [token < valid[:, s : s + 1]] * 4
        w = weight_of(jnp.concatenate(scores, axis=0))
        w = jnp.where(jnp.concatenate(live, axis=0), w, 0.0)
        t = jnp.sum(w, axis=1, keepdims=True)
        wb = w.astype(BF)
        fetch(n, v_hbm, v, v_sem).wait()
        for i, s in enumerate(slots):
            p = prompt[s, 0]
            m = jnp.dot(wb[32 * i : 32 * i + 32], v[s], preferred_element_type=F32)
            acc[p] += jnp.concatenate(
                [m[0:8, :HEAD], m[8:16, :HEAD], m[16:24, HEAD:], m[24:32, HEAD:]], axis=1
            )
            sums = jnp.zeros((BEAMS, HEAD), F32)
            for j in range(4):
                sums = jnp.where(lane == j, t[32 * i + 8 * j : 32 * i + 8 * j + 8], sums)
            tacc[p] += sums
    out[:, :, : 4 * HEAD] = acc[...].astype(BF)
    t = tacc[...]
    high = t.astype(BF).astype(F32)
    upper = lax.broadcasted_iota(jnp.int32, t.shape, 2) < 4
    out[:, :, 4 * HEAD :] = jnp.where(upper, high, t - high).astype(BF)


def fold_rows(part, out, rows):
    for t in range(FOLD):
        rows[pl.ds(t, 8, stride=FOLD), :] = part(t) if t < TILES else jnp.zeros((8, HEAD), F32)
    for r in range(8):
        out[r] = rows[r * FOLD : (r + 1) * FOLD, :].astype(BF)


def project(got, q, fresh_k, fresh_v, wo, out, rows):
    total = got[0].astype(F32)
    for i in range(1, PAGES):
        total += got[i].astype(F32)
    heads = []
    for h in range(4):
        k = h // 2
        hs, ks = slice(h * HEAD, (h + 1) * HEAD), slice(k * HEAD, (k + 1) * HEAD)
        raw = jnp.sum(q[:, hs].astype(F32) * fresh_k[:, ks].astype(F32), axis=1, keepdims=True)
        own = weight_of(raw)
        base = 4 * HEAD + h
        denominator = total[:, base : base + 1] + total[:, base + 4 : base + 5] + own
        numerator = total[:, hs] + own.astype(BF).astype(F32) * fresh_v[:, ks].astype(F32)
        heads.append(numerator / denominator)
    attention = jnp.concatenate(heads, axis=1).astype(BF)

    step = 512
    terms = [dot_nt(attention, wo[lo : lo + step, :]) for lo in range(0, D, step)]

    def part(t):
        lo = t * HEAD % step
        return terms[t * HEAD // step][:, lo : lo + HEAD]

    fold_rows(part, out, rows)


def total_of(got, count):
    total = got[0].astype(F32)
    for i in range(1, count):
        total += got[i].astype(F32)
    return total


def unit(v):
    square = jnp.sum(jnp.sum(v * v, axis=1, keepdims=True), axis=0, keepdims=True)
    return v * lax.rsqrt(square * (1.0 / D) + norm_eps)


def folded(v):
    return jnp.concatenate([v[...].astype(F32), jnp.zeros((FOLD - TILES, HEAD), F32)], axis=0)


def enter(got, stream, gain_a, gain_f, residual, spread):
    r = folded(stream) + unit(total_of(got, Y * C)) * folded(gain_a)
    residual[...] = r
    normed = (unit(r) * folded(gain_f)).astype(BF)
    for i in range(Z):
        spread[i] = normed


def widen(got, out, rows):
    for z in range(Z):
        rows[z * FOLD : (z + 1) * FOLD, :] = got[z].astype(F32)
    for t in range(TILES):
        part = rows[pl.ds(t, 8, stride=FOLD), :].astype(BF)
        for i in range(X * Y):
            out[i, :, t * HEAD : (t + 1) * HEAD] = part


def feed(x, g0, l0, g1, l1, d0, d1_hbm, out, d1, sem):
    late = pltpu.make_async_copy(d1_hbm, d1, sem)
    late.start()
    rows = x[...]

    def hidden(g, l):
        gate = dot_nt(rows, g[...])
        return (jax.nn.gelu(gate, approximate=True) * dot_nt(rows, l[...])).astype(BF)

    h0, h1 = hidden(g0, l0), hidden(g1, l1)
    late.wait()
    step = 512
    for c in range(0, D, step):
        cut = slice(c, c + step)
        y = jnp.dot(h0, d0[:, cut], preferred_element_type=F32)
        y += jnp.dot(h1, d1[:, cut], preferred_element_type=F32)
        out[:, cut] = y.astype(BF)


def gather_sum(got, out, rows):
    def part(t):
        cut = slice(t * HEAD, (t + 1) * HEAD)
        total = got[0, :, cut].astype(F32)
        for i in range(1, X * Y):
            total += got[i, :, cut].astype(F32)
        return total

    fold_rows(part, out, rows)


def leave(got, residual, gain, out):
    value = residual[...] + unit(total_of(got, Z)) * folded(gain)
    for t in range(TILES):
        out[:, t * HEAD : (t + 1) * HEAD] = value[t : t + 1].astype(BF)


def index(lengths, first, tables, parents, prompt, valid):
    rows = tables.shape[1]
    lane = lax.broadcasted_iota(jnp.int32, tables.shape, 1)
    block = lax.broadcasted_iota(jnp.int32, tables.shape, 0)
    owner = lane // BEAMS
    length = jnp.zeros(tables.shape, jnp.int32)
    for p in range(lengths.shape[0]):
        length = jnp.where(owner == p, lengths[p], length)
    tokens = jnp.clip(length - PAGE * block, 0, PAGE)
    table = tables[...]
    held = jnp.concatenate(
        [
            jnp.sum(jnp.where(table == first[0] + s, tokens, 0), axis=0, keepdims=True)
            for s in range(SLOTS)
        ],
        axis=0,
    )
    owners = lax.broadcasted_iota(jnp.int32, held.shape, 1) // BEAMS
    prompt[...] = jnp.max(jnp.where(held > 0, owners, 0), axis=1, keepdims=True)
    below = lax.broadcasted_iota(jnp.int32, (rows, rows), 0)
    chosen = jnp.where(below == parents[...], 1.0, 0.0).astype(BF)
    mine = jnp.dot(held.astype(F32).astype(BF), chosen, preferred_element_type=F32)
    beam = jnp.where(lane % BEAMS == block, 1.0, 0.0).astype(BF)
    valid[...] = dot_nt(beam, mine.astype(BF)).astype(jnp.int32)


def exchange(blocks, axes):
    return lax.all_to_all(blocks, axes, 0, 0, tiled=True)


def stay(v):
    return pltpu.with_memory_space_constraint(v, HBM)


def shaped(*shape, dtype=BF):
    return jax.ShapeDtypeStruct(shape, dtype)


def layer(
    queries,
    fresh_token_keys,
    fresh_token_values,
    paged_keys,
    paged_values,
    block_tables,
    parents,
    prompt_lengths,
    stream,
    output_matrix,
    attention_gain,
    feedforward_gain,
    gate_matrix,
    linear_matrix,
    down_matrix,
    closing_gain,
):
    gate_other, linear_other, down_other = (
        lax.ppermute(m, "c", [(0, 1), (1, 0)])
        for m in (gate_matrix, linear_matrix, down_matrix)
    )
    all_queries = exchange(jnp.broadcast_to(queries[None], (PAGES,) + queries.shape), ("z", "x"))
    page_id = lax.axis_index("z") * X + lax.axis_index("x")
    prompt, valid = kernel(
        index,
        (shaped(SLOTS, 1, dtype=jnp.int32), shaped(BEAMS, SLOTS, dtype=jnp.int32)),
        (SMEM, SMEM, VMEM, VMEM),
    )(prompt_lengths, (page_id * SLOTS).reshape(1), block_tables.T, parents.reshape(1, -1))
    stream, gain_a, gain_f, gain_c = (
        v.reshape(TILES, HEAD) for v in (stream, attention_gain, feedforward_gain, closing_gain)
    )
    all_queries, stream = lax.optimization_barrier((all_queries, stream))

    pages = pltpu.VMEM(paged_keys.shape, BF)
    batches = pltpu.SemaphoreType.DMA((SLOTS // BATCH,))
    sent = kernel(
        attend,
        shaped(PAGES, BEAMS, 5 * HEAD),
        (SMEM, VMEM, VMEM, HBM, HBM),
        [
            pages,
            pages,
            pltpu.VMEM((PAGES, BEAMS, 4 * HEAD), F32),
            pltpu.VMEM((PAGES, BEAMS, HEAD), F32),
            batches,
            batches,
        ],
        8,
    )(prompt, valid, all_queries, stay(paged_keys), stay(paged_values))
    got = exchange(sent, ("z", "x"))
    rows = [pltpu.VMEM((8 * FOLD, HEAD), F32)]
    blocks = shaped(8, FOLD, HEAD)
    sent = kernel(
        project,
        blocks,
        (VMEM,) * 5,
        rows,
        8,
    )(got, queries, fresh_token_keys, fresh_token_values, output_matrix)
    sent, gate_other, linear_other, down_other = lax.optimization_barrier(
        (sent, gate_other, linear_other, down_other)
    )
    got = exchange(sent, ("y", "c"))
    residual, sent = kernel(
        enter, (shaped(FOLD, HEAD, dtype=F32), blocks), (VMEM,) * 4
    )(got, stream, gain_a, gain_f)
    got = exchange(sent, "z")
    sent = kernel(widen, shaped(X * Y, Z, D), (VMEM,), rows)(got)
    got = exchange(sent, ("x", "y")).reshape(X * Y * Z, D)
    late = [pltpu.VMEM(down_matrix.shape, BF), pltpu.SemaphoreType.DMA(())]
    sent = kernel(feed, shaped(X * Y * Z, D), (VMEM,) * 6 + (HBM,), late, 16)(
        got, gate_matrix, linear_matrix, gate_other, linear_other, down_matrix, down_other
    )
    got = exchange(sent.reshape(X * Y, Z, D), ("x", "y"))
    sent = kernel(gather_sum, blocks, (VMEM,), rows)(got)
    got = exchange(sent, "z")
    return kernel(leave, shaped(1, D), (VMEM,) * 3)(got, residual, gain_c)


def solution(mesh):
    torus = Mesh(mesh.devices.reshape(Z, X, Y, C), ("z", "x", "y", "c"))
    page, feat, both = ("z", "x"), ("y", "c"), ("z", "x", "y", "c")
    placed = (
        P(page, feat),
        P(page, feat),
        P(page, feat),
        P(page, None, feat),
        P(page, None, feat),
        P(),
        P(),
        P(),
        P(both, None),
        P(None, feat),
        P(),
        P(),
        P(both, None),
        P(both, None),
        P(both, None),
        P(),
    )
    return jax.shard_map(
        layer, mesh=torus, in_specs=placed, out_specs=P(both, None), check_vma=False
    )
```

```python
import jax
import jax.numpy as jnp
from jax import lax
from jax.experimental import pallas as pl
from jax.experimental.pallas import tpu as pltpu
from jax.sharding import Mesh, PartitionSpec as P

HEAD = 128
ROOT_SCALE = 12.0
SOFTCAP = 50.0
BEAMS = 8
Z, X, Y, C = 8, 4, 4, 2
PAGES = Z * X
D = 4608
TILES = D // HEAD
FOLD = 40
SLOTS = 16
PAGE = 256
BATCH = 8
BF, F32 = jnp.bfloat16, jnp.float32
VMEM, SMEM, HBM = pltpu.VMEM, pltpu.SMEM, pltpu.HBM

norm_eps = 1e-06


def kernel(body, outs, spaces, scratch=(), mib=4):
    return pl.pallas_call(
        body,
        out_shape=outs,
        in_specs=[pl.BlockSpec(memory_space=m) for m in spaces],
        out_specs=jax.tree.map(lambda _: pl.BlockSpec(memory_space=VMEM), outs),
        scratch_shapes=list(scratch),
        compiler_params=pltpu.CompilerParams(vmem_limit_bytes=mib << 20),
    )


def weight_of(raw):
    return jnp.exp(SOFTCAP * jnp.tanh(raw * (1.0 / (ROOT_SCALE * SOFTCAP))))


def dot_nt(a, b):
    return lax.dot_general(a, b, (((1,), (1,)), ((), ())), preferred_element_type=F32)


def attend(prompt, valid, q, k_hbm, v_hbm, out, k, v, acc, tacc, k_sem, v_sem):
    def fetch(n, hbm, buf, sem):
        some = pl.ds(n * BATCH, BATCH)
        return pltpu.make_async_copy(hbm.at[some], buf.at[some], sem.at[n])

    for n in range(SLOTS // BATCH):
        fetch(n, k_hbm, k, k_sem).start()
        fetch(n, v_hbm, v, v_sem).start()
    acc[...] = jnp.zeros_like(acc)
    tacc[...] = jnp.zeros_like(tacc)
    token = lax.broadcasted_iota(jnp.int32, (BEAMS, PAGE), 1)
    lane = lax.broadcasted_iota(jnp.int32, (BEAMS, HEAD), 1) % 4
    blank = jnp.zeros((2 * BEAMS, HEAD), F32)
    for n in range(SLOTS // BATCH):
        slots = range(n * BATCH, (n + 1) * BATCH)
        fetch(n, k_hbm, k, k_sem).wait()
        scores, live = [], []
        for s in slots:
            queries = q[prompt[s, 0]].astype(F32)
            heads = [queries[:, i * HEAD : (i + 1) * HEAD] for i in range(4)]
            left = jnp.concatenate([heads[0], heads[1], blank], axis=0)
            right = jnp.concatenate([blank, heads[2], heads[3]], axis=0)
            scores.append(dot_nt(jnp.concatenate([left, right], axis=1).astype(BF), k[s]))
            live += [token < valid[:, s : s + 1]] * 4
        w = weight_of(jnp.concatenate(scores, axis=0))
        w = jnp.where(jnp.concatenate(live, axis=0), w, 0.0)
        t = jnp.sum(w, axis=1, keepdims=True)
        wb = w.astype(BF)
        fetch(n, v_hbm, v, v_sem).wait()
        for i, s in enumerate(slots):
            p = prompt[s, 0]
            m = jnp.dot(wb[32 * i : 32 * i + 32], v[s], preferred_element_type=F32)
            acc[p] += jnp.concatenate(
                [m[0:8, :HEAD], m[8:16, :HEAD], m[16:24, HEAD:], m[24:32, HEAD:]], axis=1
            )
            sums = jnp.zeros((BEAMS, HEAD), F32)
            for j in range(4):
                sums = jnp.where(lane == j, t[32 * i + 8 * j : 32 * i + 8 * j + 8], sums)
            tacc[p] += sums
    out[:, :, : 4 * HEAD] = acc[...].astype(BF)
    t = tacc[...]
    high = t.astype(BF).astype(F32)
    upper = lax.broadcasted_iota(jnp.int32, t.shape, 2) < 4
    out[:, :, 4 * HEAD :] = jnp.where(upper, high, t - high).astype(BF)


def fold_rows(part, out, rows):
    for t in range(FOLD):
        rows[pl.ds(t, 8, stride=FOLD), :] = part(t) if t < TILES else jnp.zeros((8, HEAD), F32)
    for r in range(8):
        out[r] = rows[r * FOLD : (r + 1) * FOLD, :].astype(BF)


def project(got, q, fresh_k, fresh_v, wo, out, rows):
    total = got[0].astype(F32)
    for i in range(1, PAGES):
        total += got[i].astype(F32)
    heads = []
    for h in range(4):
        k = h // 2
        hs, ks = slice(h * HEAD, (h + 1) * HEAD), slice(k * HEAD, (k + 1) * HEAD)
        raw = jnp.sum(q[:, hs].astype(F32) * fresh_k[:, ks].astype(F32), axis=1, keepdims=True)
        own = weight_of(raw)
        base = 4 * HEAD + h
        denominator = total[:, base : base + 1] + total[:, base + 4 : base + 5] + own
        numerator = total[:, hs] + own.astype(BF).astype(F32) * fresh_v[:, ks].astype(F32)
        heads.append(numerator / denominator)
    attention = jnp.concatenate(heads, axis=1).astype(BF)

    step = 512
    terms = [dot_nt(attention, wo[lo : lo + step, :]) for lo in range(0, D, step)]

    def part(t):
        lo = t * HEAD % step
        return terms[t * HEAD // step][:, lo : lo + HEAD]

    fold_rows(part, out, rows)


def total_of(got, count):
    total = got[0].astype(F32)
    for i in range(1, count):
        total += got[i].astype(F32)
    return total


def unit(v):
    square = jnp.sum(jnp.sum(v * v, axis=1, keepdims=True), axis=0, keepdims=True)
    return v * lax.rsqrt(square * (1.0 / D) + norm_eps)


def folded(v):
    return jnp.concatenate([v[...].astype(F32), jnp.zeros((FOLD - TILES, HEAD), F32)], axis=0)


def enter(got, stream, gain_a, gain_f, residual, spread):
    r = folded(stream) + unit(total_of(got, Y * C)) * folded(gain_a)
    residual[...] = r
    normed = (unit(r) * folded(gain_f)).astype(BF)
    for i in range(Z):
        spread[i] = normed


def unfold(got, out, rows):
    for z in range(Z):
        rows[z * FOLD : (z + 1) * FOLD, :] = got[z].astype(F32)
    for t in range(TILES):
        out[:, t * HEAD : (t + 1) * HEAD] = rows[pl.ds(t, 8, stride=FOLD), :].astype(BF)


def bundle(own, one, two, three, out):
    for i, part in enumerate((own, one, two, three)):
        out[i] = part[...]


def feed(homes, b0, b1, b2, b3, g0, l0, g1, l1, d0, d1_hbm, out, d1, sem, x):
    late = pltpu.make_async_copy(d1_hbm, d1, sem)
    late.start()
    for i, b in enumerate((b0, b1, b2, b3)):
        x[i * 4 * Z : (i + 1) * 4 * Z] = b[...]
    rows = x[...]

    def hidden(g, l):
        gate = dot_nt(rows, g[...])
        return (jax.nn.gelu(gate, approximate=True) * dot_nt(rows, l[...])).astype(BF)

    h0, h1 = hidden(g0, l0), hidden(g1, l1)
    late.wait()
    step = 512
    for c in range(0, D, step):
        cut = slice(c, c + step)
        y = jnp.dot(h0, d0[:, cut], preferred_element_type=F32)
        y += jnp.dot(h1, d1[:, cut], preferred_element_type=F32)
        for i in range(X * Y):
            out[homes[i], :, cut] = y[i * Z : (i + 1) * Z].astype(BF)


def gather_sum(got, out, rows):
    def part(t):
        cut = slice(t * HEAD, (t + 1) * HEAD)
        total = got[0, :, cut].astype(F32)
        for i in range(1, X * Y):
            total += got[i, :, cut].astype(F32)
        return total

    fold_rows(part, out, rows)


def leave(got, residual, gain, out):
    value = residual[...] + unit(total_of(got, Z)) * folded(gain)
    for t in range(TILES):
        out[:, t * HEAD : (t + 1) * HEAD] = value[t : t + 1].astype(BF)


def index(lengths, first, tables, parents, prompt, valid):
    rows = tables.shape[1]
    lane = lax.broadcasted_iota(jnp.int32, tables.shape, 1)
    block = lax.broadcasted_iota(jnp.int32, tables.shape, 0)
    owner = lane // BEAMS
    length = jnp.zeros(tables.shape, jnp.int32)
    for p in range(lengths.shape[0]):
        length = jnp.where(owner == p, lengths[p], length)
    tokens = jnp.clip(length - PAGE * block, 0, PAGE)
    table = tables[...]
    held = jnp.concatenate(
        [
            jnp.sum(jnp.where(table == first[0] + s, tokens, 0), axis=0, keepdims=True)
            for s in range(SLOTS)
        ],
        axis=0,
    )
    owners = lax.broadcasted_iota(jnp.int32, held.shape, 1) // BEAMS
    prompt[...] = jnp.max(jnp.where(held > 0, owners, 0), axis=1, keepdims=True)
    below = lax.broadcasted_iota(jnp.int32, (rows, rows), 0)
    chosen = jnp.where(below == parents[...], 1.0, 0.0).astype(BF)
    mine = jnp.dot(held.astype(F32).astype(BF), chosen, preferred_element_type=F32)
    beam = jnp.where(lane % BEAMS == block, 1.0, 0.0).astype(BF)
    valid[...] = dot_nt(beam, mine.astype(BF)).astype(jnp.int32)


def shift(block, first, distance):
    pairs = []
    for n in range(Z * X * Y * C):
        c, y, x, z = n % C, n // C % Y, n // (C * Y) % X, n // (C * Y * X)
        if (c == 0) == first:
            x = (x + distance) % X
        else:
            y = (y + distance) % Y
        pairs.append((n, ((z * X + x) * Y + y) * C + c))
    return lax.ppermute(block, ("z", "x", "y", "c"), pairs)


def shifts(blocks, first, sign):
    moved = {}
    for d in (2, 1, 3):
        moved[d] = shift(blocks[d], first, sign * d)
    return moved[1], moved[2], moved[3]


def exchange(blocks, axes):
    return lax.all_to_all(blocks, axes, 0, 0, tiled=True)


def stay(v):
    return pltpu.with_memory_space_constraint(v, HBM)


def shaped(*shape, dtype=BF):
    return jax.ShapeDtypeStruct(shape, dtype)


def layer(
    queries,
    fresh_token_keys,
    fresh_token_values,
    paged_keys,
    paged_values,
    block_tables,
    parents,
    prompt_lengths,
    stream,
    output_matrix,
    attention_gain,
    feedforward_gain,
    gate_matrix,
    linear_matrix,
    down_matrix,
    closing_gain,
):
    gate_other, linear_other, down_other = (
        lax.ppermute(m, "c", [(0, 1), (1, 0)])
        for m in (gate_matrix, linear_matrix, down_matrix)
    )
    all_queries = exchange(jnp.broadcast_to(queries[None], (PAGES,) + queries.shape), ("z", "x"))
    page_id = lax.axis_index("z") * X + lax.axis_index("x")
    prompt, valid = kernel(
        index,
        (shaped(SLOTS, 1, dtype=jnp.int32), shaped(BEAMS, SLOTS, dtype=jnp.int32)),
        (SMEM, SMEM, VMEM, VMEM),
    )(prompt_lengths, (page_id * SLOTS).reshape(1), block_tables.T, parents.reshape(1, -1))
    step = jnp.arange(X * Y, dtype=jnp.int32)
    one, two = step % 4, step // 4
    even = lax.axis_index("c") == 0
    home_x = (lax.axis_index("x") - jnp.where(even, one, two)) % X
    homes = home_x * Y + (lax.axis_index("y") - jnp.where(even, two, one)) % Y
    stream, gain_a, gain_f, gain_c = (
        v.reshape(TILES, HEAD) for v in (stream, attention_gain, feedforward_gain, closing_gain)
    )
    all_queries, stream, homes = lax.optimization_barrier((all_queries, stream, homes))

    pages = pltpu.VMEM(paged_keys.shape, BF)
    batches = pltpu.SemaphoreType.DMA((SLOTS // BATCH,))
    sent = kernel(
        attend,
        shaped(PAGES, BEAMS, 5 * HEAD),
        (SMEM, VMEM, VMEM, HBM, HBM),
        [
            pages,
            pages,
            pltpu.VMEM((PAGES, BEAMS, 4 * HEAD), F32),
            pltpu.VMEM((PAGES, BEAMS, HEAD), F32),
            batches,
            batches,
        ],
        8,
    )(prompt, valid, all_queries, stay(paged_keys), stay(paged_values))
    got = exchange(sent, ("z", "x"))
    rows = [pltpu.VMEM((8 * FOLD, HEAD), F32)]
    blocks = shaped(8, FOLD, HEAD)
    sent = kernel(
        project,
        blocks,
        (VMEM,) * 5,
        rows,
        8,
    )(got, queries, fresh_token_keys, fresh_token_values, output_matrix)
    sent, gate_other, linear_other, down_other = lax.optimization_barrier(
        (sent, gate_other, linear_other, down_other)
    )
    got = exchange(sent, ("y", "c"))
    residual, sent = kernel(
        enter, (shaped(FOLD, HEAD, dtype=F32), blocks), (VMEM,) * 4
    )(got, stream, gain_a, gain_f)
    got = exchange(sent, "z")
    block = kernel(unfold, shaped(Z, D), (VMEM,), rows)(got)
    near = shifts((block,) * 4, True, 1)
    sent = kernel(bundle, shaped(4, Z, D), (VMEM,) * 4)(block, *near).reshape(4 * Z, D)
    far = shifts((sent,) * 4, False, 1)
    late = [
        pltpu.VMEM(down_matrix.shape, BF),
        pltpu.SemaphoreType.DMA(()),
        pltpu.VMEM((X * Y * Z, D), BF),
    ]
    spaces = (SMEM,) + (VMEM,) * 9 + (HBM,)
    sent = kernel(feed, shaped(X * Y, Z, D), spaces, late, 16)(
        homes,
        sent,
        *far,
        gate_matrix,
        linear_matrix,
        gate_other,
        linear_other,
        down_matrix,
        down_other,
    )
    got = exchange(sent, ("x", "y"))
    sent = kernel(gather_sum, blocks, (VMEM,), rows)(got)
    got = exchange(sent, "z")
    return kernel(leave, shaped(1, D), (VMEM,) * 3)(got, residual, gain_c)


def solution(mesh):
    torus = Mesh(mesh.devices.reshape(Z, X, Y, C), ("z", "x", "y", "c"))
    page, feat, both = ("z", "x"), ("y", "c"), ("z", "x", "y", "c")
    placed = (
        P(page, feat),
        P(page, feat),
        P(page, feat),
        P(page, None, feat),
        P(page, None, feat),
        P(),
        P(),
        P(),
        P(both, None),
        P(None, feat),
        P(),
        P(),
        P(both, None),
        P(both, None),
        P(both, None),
        P(),
    )
    return jax.shard_map(
        layer, mesh=torus, in_specs=placed, out_specs=P(both, None), check_vma=False
    )
```
